128 devices in a mesh: stream: 4 (over x), seq: 32 (over z, y, core).
Axes of the slice: x: 4, y: 4, z: 4, core: 2. Of those that a mesh axis runs over, the one named last changes fastest.
Arguments:
- conv_input: bfloat16 [4, 131072, 1280], P('stream', 'seq'), may hold values from -6 to 6
- conv_weight: float32 [4, 1280], replicated, may hold values from -3 to 3
- conv_bias: float32 [1280], replicated, may hold values from -1 to 1
- step_size: float32 [4, 16, 131072], P('stream', None, 'seq'), may hold values from 0.0005 to 0.005
- log_decay: float32 [4, 16, 131072], P('stream', None, 'seq'), as said below
- skip_gain: float32 [16], replicated, may hold values from 0.5 to 1.5
- doc_bounds: int32 [4, 128], P('stream'), may hold values from 1 to 131072, as said below
- doc_owner: int32 [4, 128], P('stream'), may hold values from 0 to 3, as said below
Outputs:
- mixed_out: bfloat16 [4, 131072, 1024], P('stream', 'seq')
- handoff_ssm: float32 [4, 32, 4, 2, 16, 64, 128], P('stream', 'seq')
- handoff_conv: bfloat16 [4, 32, 4, 2, 3, 1280], P('stream', 'seq')
The draws below stay inside these ranges and needn't reach their ends.
Inputs may be any that keep to these rules, and one draw needn't show every extreme that they name: `doc_bounds`: each row rises and never falls; the real documents of a stream end at 131072, after which every entry equals 131072. At most 4 real documents have their last position in one run of 4096 positions starting at a multiple of 4096. `doc_owner`: among the real documents whose last positions lie in one such run of one stream, no owner is named more than 2 times. `log_decay`: never positive.
All inputs are finite; a program needn't handle non-finite values.
Results may differ from the reference program's by a relative error of at most 0.006.
Values may be sent and summed in bfloat16 or wider, within the bound.
A program may use at most 256 MiB of HBM per device.

```python
import math
import jax
import jax.numpy as jnp
from jax import lax

H = 16
P_SIZE = 64
N = 128
CONV = 4
SPAN = 256
EMAX = 4
CAP = 2
TOK_DEV = 4096
CH = 1280
PROMPT_STREAMS = 4
STREAM_LENGTH = 131072
NB = 128
N_STREAM = 4
N_SEQ = 32


def shared_docs(key):
    key_sequence = jax.random.split(jax.random.fold_in(key, 11), 7)
    shard_ids = jnp.arange(N_SEQ)
    run_length = N_SEQ // 2 + 1
    run_start = jax.random.randint(key_sequence[6], (PROMPT_STREAMS, 1), 1, N_SEQ - run_length)
    in_run = (shard_ids[None, :] >= run_start) & (shard_ids[None, :] < run_start + run_length)
    end_counts = jax.random.randint(key_sequence[0], (PROMPT_STREAMS, N_SEQ), 1, EMAX + 1)
    full_shard = run_start - 1
    end_counts = jnp.where(shard_ids[None, :] == full_shard, EMAX, end_counts)
    end_counts = jnp.where(in_run, 0, end_counts)
    pick_keys = jax.random.split(key_sequence[2], PROMPT_STREAMS * N_SEQ)
    offsets = jax.vmap(lambda one_key: jnp.sort(jax.random.permutation(one_key, TOK_DEV)[:EMAX]))(pick_keys)
    offsets = offsets.reshape(PROMPT_STREAMS, N_SEQ, EMAX)
    slot_ids = jnp.arange(EMAX)
    offsets = jnp.where((shard_ids[None, :, None] == N_SEQ - 1) & (slot_ids[None, None, :] == EMAX - 1), TOK_DEV - 1, offsets)
    used = slot_ids[None, None, :] >= EMAX - end_counts[:, :, None]
    end_points = jnp.where(used, shard_ids[None, :, None] * TOK_DEV + offsets + 1, STREAM_LENGTH)
    order_keys = jax.random.split(key_sequence[3], PROMPT_STREAMS * N_SEQ)
    shuffled = jax.vmap(lambda one_key: jax.random.permutation(one_key, EMAX))(order_keys).reshape(PROMPT_STREAMS, N_SEQ, EMAX)
    base_owner = jax.random.randint(key_sequence[4], (PROMPT_STREAMS, N_SEQ), 0, N_STREAM)
    full_owner = jax.random.randint(key_sequence[5], (), 0, N_STREAM)
    base_owner = jnp.where(shard_ids[None, :] == full_shard, full_owner, base_owner)
    owner_of = (base_owner[:, :, None] + shuffled // CAP) % N_STREAM
    flat_ends = end_points.reshape(PROMPT_STREAMS, NB).astype(jnp.int32)
    flat_owner = owner_of.reshape(PROMPT_STREAMS, NB).astype(jnp.int32)
    sorted_ends, sorted_owner = lax.sort((flat_ends, flat_owner), dimension=1, is_stable=True, num_keys=1)
    return (sorted_ends.astype(jnp.int32), sorted_owner.astype(jnp.int32))


def draw_doc_bounds(key, part):
    return shared_docs(key)[0]


def draw_doc_owner(key, part):
    return shared_docs(key)[1]


def draw_log_decay(key, part):
    key_sequence = jax.random.split(jax.random.fold_in(key, 5), 8)
    fast_count = jax.random.randint(key_sequence[0], (), max(1, H // 4), max(2, min(H, 3 * H // 4 + 1)))
    head_order = jax.random.permutation(key_sequence[1], H)
    is_fast = head_order < fast_count
    fast_rate = jnp.exp(jax.random.uniform(key_sequence[2], (H,), jnp.float32, math.log(1.0 / 50.0), math.log(1.0 / 30.0)))
    slow_rate = jax.random.uniform(key_sequence[3], (H,), jnp.float32, 0.05, 0.5) / STREAM_LENGTH
    decay_rate = jnp.where(is_fast, fast_rate, slow_rate)
    shard_factor = jnp.exp(jax.random.uniform(key_sequence[4], (PROMPT_STREAMS, H, N_SEQ), jnp.float32, math.log(0.5), math.log(2.0)))
    shard_factor = jnp.repeat(shard_factor, TOK_DEV, axis=2)
    token_factor = jnp.exp(jax.random.uniform(key_sequence[5], (PROMPT_STREAMS, H, STREAM_LENGTH), jnp.float32, math.log(0.5), math.log(2.0)))
    decay_factors = -decay_rate[None, :, None] * shard_factor * token_factor
    flurry_location = jax.random.randint(key_sequence[6], (PROMPT_STREAMS, 3), 0, STREAM_LENGTH)
    flurry_penalty = jax.random.uniform(key_sequence[7], (PROMPT_STREAMS, 3), jnp.float32, 0.2, 0.4)
    token_positions = jnp.arange(STREAM_LENGTH)
    flurry_discard = jnp.sum(jnp.where(token_positions[None, :, None] == flurry_location[:, None, :], jnp.log1p(-flurry_penalty)[:, None, :], 0.0), axis=2)
    return (decay_factors + flurry_discard[:, None, :]).astype(jnp.float32)


def block_levels(rng, extent, cuts, least, largest):
    def one(axis_at, blocks):
        draws = jax.random.uniform(jax.random.fold_in(jax.random.fold_in(rng, 6), axis_at), (blocks,), jnp.float32, least / len(cuts), largest / len(cuts))
        return jnp.repeat(jnp.exp(draws), extent[axis_at] // blocks).reshape((-1,) + (1,) * (len(extent) - axis_at - 1))

    level = one(*cuts[0])
    for cut in cuts[1:]:
        level = level * one(*cut)
    return level


def noise(stream_key, dims, scale, most, cuts=(), held_as=jnp.bfloat16):
    gain = block_levels(stream_key, dims, cuts, -0.22, 0.18) if cuts else 1.0
    result = jax.random.normal(stream_key, dims, jnp.float32) * scale * gain
    return jnp.minimum(jnp.maximum(result, -most), most).astype(held_as)


def setup_inputs(seed: int = 0) -> dict:
    seeds = jax.random.split(jax.random.key(seed), 9)
    conv_input = noise(seeds[0], (PROMPT_STREAMS, STREAM_LENGTH, CH), 1.0, 6.0, ((0, 4), (1, 32)))
    conv_weight = noise(seeds[1], (CONV, CH), CONV ** -0.5, 3.0, (), jnp.float32)
    conv_bias = jnp.clip(jax.random.uniform(seeds[2], (CH,), jnp.float32, -1.0, 1.0), -1.0, 1.0)
    step_size = jnp.clip(jnp.exp(math.log(0.005) - 2.30258502 * jax.random.uniform(seeds[3], (PROMPT_STREAMS, H, STREAM_LENGTH), jnp.float32) ** block_levels(seeds[3], (PROMPT_STREAMS, H, STREAM_LENGTH), ((0, 4), (2, 32)), -0.2, 0.2)), 0.0005, 0.005)
    log_decay = draw_log_decay(jax.random.fold_in(seeds[8], 71), 0)
    skip_gain = jnp.clip(jax.random.uniform(seeds[5], (H,), jnp.float32, 0.5, 1.5), 0.5, 1.5)
    doc_bounds = draw_doc_bounds(jax.random.fold_in(seeds[8], 71), 0)
    doc_owner = draw_doc_owner(jax.random.fold_in(seeds[8], 71), 0)
    return dict(conv_input=conv_input, conv_weight=conv_weight, conv_bias=conv_bias, step_size=step_size, log_decay=log_decay, skip_gain=skip_gain, doc_bounds=doc_bounds, doc_owner=doc_owner)


def split_product(c_rows, state):
    state_hi = state.astype(jnp.bfloat16)
    state_lo = (state - state_hi.astype(jnp.float32)).astype(jnp.bfloat16)
    c_wide = c_rows.astype(jnp.float32)
    first = jnp.einsum("tn,hpn->thp", c_wide, state_hi.astype(jnp.float32))
    second = jnp.einsum("tn,hpn->thp", c_wide, state_lo.astype(jnp.float32))
    return first + second


def conv_mix(conv_rows, doc_ids, conv_weight, conv_bias):
    values = conv_rows.astype(jnp.float32)
    mixed_sum = conv_bias[None, :] + conv_weight[0][None, :] * values
    for lag_step in range(1, CONV):
        moved_rows = jnp.concatenate([jnp.zeros((lag_step, values.shape[1]), jnp.float32), values[:-lag_step]], 0)
        moved_doc = jnp.concatenate([jnp.full((lag_step,), -1, jnp.int32), doc_ids[:-lag_step]], 0)
        mixed_sum = mixed_sum + conv_weight[lag_step][None, :] * jnp.where((moved_doc == doc_ids)[:, None], moved_rows, 0.0)
    return jax.nn.silu(mixed_sum).astype(jnp.bfloat16)


def span_output(x_span, b_span, c_span, dt_span, cum_decay, doc_span, prev_doc, state_in, skip_gain):
    row_count = doc_span.shape[0]
    head_count = dt_span.shape[0]
    scores = jnp.dot(c_span, b_span.T, preferred_element_type=jnp.float32)
    position = jnp.arange(row_count)
    causal = (position[:, None] >= position[None, :]) & (doc_span[:, None] == doc_span[None, :])
    spread = cum_decay[:, :, None] - cum_decay[:, None, :]
    weights = jnp.where(causal[None], jnp.exp(jnp.where(causal[None], spread, 0.0)) * scores[None] * dt_span[:, None, :], 0.0).astype(jnp.bfloat16)
    head_rows = x_span.reshape(row_count, head_count, -1)
    inner_part = jnp.einsum("hts,shp->thp", weights.astype(jnp.float32), head_rows.astype(jnp.float32))
    entry_gate = jnp.where((doc_span == prev_doc)[None, :], jnp.exp(cum_decay), 0.0)
    outer_part = split_product(c_span, state_in) * entry_gate.T[:, :, None]
    summed = inner_part + outer_part + skip_gain[None, :, None] * head_rows.astype(jnp.float32)
    return summed.reshape(row_count, -1)


def partial_state(x_span, b_span, dt_span, cum_decay, doc_span, last_row, doc_key):
    row_count = doc_span.shape[0]
    head_count = dt_span.shape[0]
    kept_rows = (jnp.arange(row_count) <= last_row) & (doc_span == doc_key)
    scaled = jnp.where(kept_rows[None, :], jnp.exp(cum_decay[:, last_row][:, None] - cum_decay) * dt_span, 0.0)
    loaded = (scaled.T[:, :, None] * x_span.reshape(row_count, head_count, -1).astype(jnp.float32)).astype(jnp.bfloat16)
    return jnp.einsum("shp,sn->hpn", loaded.astype(jnp.float32), b_span.astype(jnp.float32))


def one_stream(conv_rows, step_rows, decay_rows, bound_row, conv_weight, conv_bias, skip_gain):
    width = H * P_SIZE
    position = jnp.arange(STREAM_LENGTH, dtype=jnp.int32)
    doc_ids = jnp.searchsorted(bound_row, position, side="right").astype(jnp.int32)
    activated = conv_mix(conv_rows, doc_ids, conv_weight, conv_bias)
    count = STREAM_LENGTH // SPAN
    x_spans = activated[:, :width].reshape(count, SPAN, width)
    b_spans = activated[:, width:width + N].reshape(count, SPAN, N)
    c_spans = activated[:, width + N:].reshape(count, SPAN, N)
    dt_spans = step_rows.reshape(H, count, SPAN).transpose(1, 0, 2)
    ld_spans = decay_rows.reshape(H, count, SPAN).transpose(1, 0, 2)
    doc_spans = doc_ids.reshape(count, SPAN)
    prev_docs = jnp.concatenate([jnp.full((1,), -1, jnp.int32), doc_spans[:-1, -1]])

    def advance(state_in, item):
        x_span, b_span, c_span, dt_span, ld_span, doc_span, prev_doc = item
        cum_decay = jnp.cumsum(ld_span, axis=1)
        out_rows = span_output(x_span, b_span, c_span, dt_span, cum_decay, doc_span, prev_doc, state_in, skip_gain)
        block_state = partial_state(x_span, b_span, dt_span, cum_decay, doc_span, SPAN - 1, doc_span[-1])
        gate = jnp.where(doc_span[-1] == prev_doc, jnp.exp(cum_decay[:, -1]), 0.0)
        return block_state + gate[:, None, None] * state_in, (out_rows.astype(jnp.bfloat16), state_in)

    start_state = jnp.zeros((H, P_SIZE, N), jnp.float32)
    _, (out_spans, state_stack) = lax.scan(advance, start_state, (x_spans, b_spans, c_spans, dt_spans, ld_spans, doc_spans, prev_docs))
    padded = jnp.concatenate([jnp.zeros((CONV - 1, conv_rows.shape[1]), jnp.bfloat16), conv_rows], 0)

    def finish(doc_index):
        end_pos = bound_row[doc_index]
        start_pos = jnp.where(doc_index > 0, bound_row[jnp.maximum(doc_index - 1, 0)], 0)
        is_real = end_pos > start_pos
        last_pos = jnp.clip(end_pos - 1, 0, STREAM_LENGTH - 1)
        block = last_pos // SPAN
        offset = last_pos % SPAN
        cum_decay = jnp.cumsum(ld_spans[block], axis=1)
        state = partial_state(x_spans[block], b_spans[block], dt_spans[block], cum_decay, doc_spans[block], offset, doc_index)
        state = state + jnp.where(prev_docs[block] == doc_index, jnp.exp(cum_decay[:, offset]), 0.0)[:, None, None] * state_stack[block]
        tail_rows = lax.dynamic_slice_in_dim(padded, last_pos + 1, CONV - 1, 0)
        tail_pos = last_pos - (CONV - 2) + jnp.arange(CONV - 1, dtype=jnp.int32)
        tail = jnp.where((tail_pos >= start_pos)[:, None], tail_rows, jnp.zeros_like(tail_rows))
        return jnp.where(is_real, state, 0.0), tail, is_real, (last_pos // TOK_DEV).astype(jnp.int32)

    finals, tails, real_docs, shard_of = lax.map(finish, jnp.arange(NB, dtype=jnp.int32))
    return out_spans.reshape(STREAM_LENGTH, width), finals, tails, real_docs, shard_of


def reference(conv_input, conv_weight, conv_bias, step_size, log_decay, skip_gain, doc_bounds, doc_owner):
    handoff_ssm = jnp.zeros((N_STREAM, N_SEQ, PROMPT_STREAMS, CAP, H, P_SIZE, N), jnp.float32)
    handoff_conv = jnp.zeros((N_STREAM, N_SEQ, PROMPT_STREAMS, CAP, CONV - 1, H * P_SIZE + 2 * N), jnp.bfloat16)
    outputs = []
    doc_index = jnp.arange(NB, dtype=jnp.int32)
    for stream in range(PROMPT_STREAMS):
        out_rows, finals, tails, real_docs, shard_of = one_stream(conv_input[stream], step_size[stream], log_decay[stream], doc_bounds[stream], conv_weight, conv_bias, skip_gain)
        outputs.append(out_rows)
        owner_row = doc_owner[stream]
        same = real_docs[None, :] & (shard_of[None, :] == shard_of[:, None]) & (owner_row[None, :] == owner_row[:, None]) & (doc_index[None, :] < doc_index[:, None])
        slot_rank = jnp.sum(same.astype(jnp.int32), axis=1).astype(jnp.int32)
        target = jnp.where(real_docs, owner_row, N_STREAM).astype(jnp.int32)
        handoff_ssm = handoff_ssm.at[target, shard_of, stream, slot_rank].set(finals, mode="drop")
        handoff_conv = handoff_conv.at[target, shard_of, stream, slot_rank].set(tails, mode="drop")
    return jnp.stack(outputs), handoff_ssm, handoff_conv
```

```python
import functools

import jax
import jax.numpy as jnp
from jax import lax
from jax.experimental import pallas as pl
from jax.experimental.pallas import tpu as pltpu
from jax.sharding import PartitionSpec as P

MESH = pl.DeviceIdType.MESH
F32 = jnp.float32
BF16 = jnp.bfloat16
T = 4096
CH = 1280
W = 1024
H = 16
N = 128
L = 64
BLK = 256
STEPS = T // BLK
NC = T // L
NSEQ = 32
NSTR = 4
PAY = 1056
BIG = 1 << 20
LOG2E = 1.4426950408889634


def dot(a, b, ca=1, cb=0):
    return lax.dot_general(a, b, (((ca,), (cb,)), ((), ())), preferred_element_type=F32)


def iota(shape, dim):
    return lax.broadcasted_iota(jnp.int32, shape, dim)


def doc_start(pos, meta):
    start = jnp.full(pos.shape, meta[13], jnp.int32)
    for n in range(4):
        start = jnp.where(pos >= meta[n], meta[n], start)
    return start


def doc_end(pos, meta):
    end = jnp.full(pos.shape, T, jnp.int32)
    for n in range(3, -1, -1):
        end = jnp.where(pos < meta[n], jnp.minimum(meta[n], T), end)
    return end


def pick(table, lane):
    return jnp.take_along_axis(table, lane, axis=1)


def left(v, s):
    return pltpu.roll(v, v.shape[1] - s, 1)


def scan_docs(bounds, owners, meta, anchor):
    for k in range(16):
        meta[k] = BIG if k < 4 else 0
    meta[13] = -anchor

    def body(k, prev):
        bound = bounds[k]

        @pl.when((bound <= anchor) & (bound > prev))
        def _():
            meta[13] = bound - anchor

        @pl.when((bound > anchor) & (bound <= anchor + T) & (bound > prev))
        def _():
            n = meta[12]
            owner = owners[k]
            rank = jnp.int32(0)
            for m in range(4):
                same = (m < n) & (meta[4 + m] == owner)
                rank = rank + jnp.where(same, 1, 0).astype(jnp.int32)
            meta[n] = bound - anchor
            meta[4 + n] = owner
            meta[8 + n] = rank
            meta[12] = n + 1

        return bound

    lax.fori_loop(0, bounds.shape[0], body, jnp.int32(0))


def decay_tables(meta, ld, dt, ldr, dtr, cols, crow, grow, gate, wide, table):
    pos = iota((1, T), 1)
    end = doc_end(pos, meta)
    wide[0:1, :] = doc_start(pos, meta)
    wide[1:2, :] = end
    for half in range(2):
        heads = slice(8 * half, 8 * half + 8)
        v = ld[heads, :] * LOG2E
        seg = jnp.where(pos + 1 < end, left(v, 1), 0.0)
        for k in range(12):
            s = 1 << k
            seg = seg + jnp.where(pos + s < end, left(seg, s), 0.0)
        whole = jnp.exp2(v[:, :1] + seg[:, :1])
        gate[heads, :] = jnp.broadcast_to(jnp.where(meta[13] < 0, whole, 0.0), (8, N))
        table[48 + 8 * half : 56 + 8 * half, :] = jnp.exp2(seg) * dt[heads, :]
    table[64:N, :] = jnp.zeros((N - 64, T), F32)

    def narrow(b, _):
        at = pl.ds(pl.multiple_of(b * N, N), N)
        place = iota((1, N), 1)
        base = b * N + place - place % L
        start = wide[0:1, at]
        end = wide[1:2, at]
        v = ld[:, at] * LOG2E
        cum = v
        suf = jnp.where(place % L + 1 < L, left(v, 1), 0.0)
        for k in range(6):
            s = 1 << k
            cum = cum + jnp.where(place % L >= s, pltpu.roll(cum, s, 1), 0.0)
            suf = suf + jnp.where(place % L + s < L, left(suf, s), 0.0)
        table[0:H, at] = cum
        table[H : 2 * H, at] = jnp.where(end >= base + L, jnp.exp2(suf) * dt[:, at], 0.0)
        table[2 * H : 3 * H, at] = jnp.where(start < base, jnp.exp2(cum), 0.0)
        cols[at, :] = table[:, at].T
        return 0

    lax.fori_loop(0, T // N, narrow, 0, unroll=4)
    first = iota((NC, 1), 0) * L
    open_block = doc_start(first + (L - 1), meta) < first
    lane = iota((NC, N), 1) % L
    for j in range(8):
        lanes = slice(j * N, (j + 1) * N)
        v = ldr[:, lanes] * LOG2E
        cum = v
        suf = jnp.where(lane + 1 < L, left(v, 1), 0.0)
        for k in range(6):
            s = 1 << k
            cum = cum + jnp.where(lane >= s, pltpu.roll(cum, s, 1), 0.0)
            suf = suf + jnp.where(lane + s < L, left(suf, s), 0.0)
        crow[j] = cum - jnp.log2(dtr[:, lanes])
        grow[j] = jnp.where(open_block, jnp.exp2(cum + suf), 0.0)


def first_kernel(
    bounds, owners, x_ref, halo, cw, cb, ld, dt, ldr, dtr,
    act, cols, crow, grow, gate, ends, sends, meta,
    xf, acc, half, wide, table, load,
):
    i = pl.program_id(0)
    anchor = lax.axis_index("seq") * T

    @pl.when(i == 0)
    def _():
        scan_docs(bounds, owners, meta, anchor)
        decay_tables(meta, ld, dt, ldr, dtr, cols, crow, grow, gate, wide, table)
        acc[...] = jnp.zeros_like(acc)
        sends[...] = jnp.zeros_like(sends)
        half[0:4, :] = cw[...] * 0.5
        half[4:5, :] = cb[...] * 0.5
        before = iota((16, 1), 0) - 16
        real = (before >= meta[13]) & (anchor > 0)
        for j in range(CH // N):
            rows = halo[:, j * N : (j + 1) * N].astype(F32)
            xf[j, 0:16, :] = jnp.where(real, rows, 0.0)

    for j in range(CH // N):
        lanes = slice(j * N, (j + 1) * N)
        xf[j, 16 : 16 + BLK, :] = x_ref[:, lanes].astype(F32)
        for r in range(0, BLK, 64):
            v = half[4:5, lanes] + half[0:1, lanes] * xf[j, 16 + r : 80 + r, :]
            for k in range(1, 4):
                v = v + half[k : k + 1, lanes] * xf[j, 16 + r - k : 80 + r - k, :]
            act[r : r + 64, lanes] = (v + v * jnp.tanh(v)).astype(BF16)

    def fix(m, _):
        doc_begin = meta[m >> 1]
        group = (doc_begin + 2 * (m & 1)) >> 4
        again = ((m & 1) == 1) & (group == doc_begin >> 4)

        @pl.when((group >> 4 == i) & jnp.logical_not(again))
        def _():
            at = pl.multiple_of((group & 15) * 16, 16)
            pos = group * 16 + iota((16, 1), 0)
            start = doc_start(pos, meta)
            for j in range(CH // N):
                lanes = slice(j * N, (j + 1) * N)
                rows = xf[j, pl.ds(at, 32), :]
                v = half[4:5, lanes] + half[0:1, lanes] * rows[16:32]
                for k in range(1, 4):
                    moved = jnp.where(pos - k >= start, rows[16 - k : 32 - k], 0.0)
                    v = v + half[k : k + 1, lanes] * moved
                act[pl.ds(at, 16), lanes] = (v + v * jnp.tanh(v)).astype(BF16)

        return 0

    touched = jnp.bool_(False)
    for n in range(4):
        touched = touched | ((meta[n] - 1) >> 8 == i) | ((meta[n] + 2) >> 8 == i)

    @pl.when(touched)
    def _():
        lax.fori_loop(0, 8, fix, 0)

    def take_tail(n, _):
        last = meta[n] - 1

        @pl.when(last >> 8 == i)
        def _():
            row = iota((32, 16 + BLK), 0)
            at = iota((32, 16 + BLK), 1) - 16 + i * BLK
            begin = jnp.where(n > 0, meta[jnp.maximum(n - 1, 0)], meta[13])
            total = jnp.zeros((32, N), F32)
            for j in range(CH // N):
                lag = row - 3 * j
                hit = (lag >= 0) & (lag < 3) & (at == last - 2 + lag) & (at >= begin)
                total = total + dot(jnp.where(hit, 1.0, 0.0).astype(BF16), xf[j].astype(BF16))
            sends[meta[8 + n], meta[4 + n], W:PAY, :] = total.astype(BF16)

        return 0

    @pl.when(touched)
    def _():
        lax.fori_loop(0, 4, take_tail, 0)

    for j in range(CH // N):
        xf[j, 0:16, :] = xf[j, BLK : BLK + 16, :]

    part = iota((L, N), 1) // L
    for r in range(0, BLK, L):
        col = cols[pl.ds(pl.multiple_of(i * BLK + r, L), L), :]
        for j in range(8):
            lanes = slice(j * N, (j + 1) * N)
            weight = pick(col, part + (2 * j + 3 * H)).astype(BF16)
            load[r : r + L, lanes] = act[r : r + L, lanes] * weight
    low = jnp.int32(0)
    high = jnp.int32(0)
    for n in range(4):
        low = low + jnp.where(meta[n] <= i * BLK, 1, 0).astype(jnp.int32)
        high = high + jnp.where(meta[n] <= i * BLK + BLK - 1, 1, 0).astype(jnp.int32)
    row = i * BLK + iota((BLK, 1), 0)

    def segment(j, _):
        begin = jnp.where(j > 0, meta[jnp.maximum(j - 1, 0)], 0)
        stop = jnp.where(j < 4, meta[jnp.minimum(j, 3)], BIG)
        kept = jnp.where((row >= begin) & (row < stop), act[:, W : W + N].astype(F32), 0.0)
        flipped = kept.astype(BF16).T
        for g in range(4):
            wide_lanes = slice(g * 2 * N, (g + 1) * 2 * N)
            acc[j, :, wide_lanes] = acc[j, :, wide_lanes] + dot(flipped, load[:, wide_lanes])
        return 0

    lax.fori_loop(low, high + 1, segment, 0)

    @pl.when(i == STEPS - 1)
    def _():
        for b in range(8):
            tile = acc[meta[12], :, b * N : (b + 1) * N].T
            ends[b * N : (b + 1) * N, :] = tile.astype(BF16)

        def put(n, _):
            for b in range(8):
                tile = acc[n, :, b * N : (b + 1) * N].T
                sends[meta[8 + n], meta[4 + n], b * N : (b + 1) * N, :] = tile.astype(BF16)
            return 0

        lax.fori_loop(0, meta[12], put, 0)


def run_first(bounds, owners, x, halo, cw, cb, ld, dt, ldr, dtr):
    smem = pl.BlockSpec(memory_space=pltpu.SMEM)
    full = lambda *shape: pl.BlockSpec(shape, lambda i: (0,) * len(shape))
    return pl.pallas_call(
        first_kernel,
        grid=(STEPS,),
        in_specs=[
            smem, smem, pl.BlockSpec((BLK, CH), lambda i: (i, 0)), full(16, CH), full(4, CH),
            full(1, CH), full(H, T), full(H, T), full(NC, W), full(NC, W),
        ],
        out_specs=[
            pl.BlockSpec((BLK, CH), lambda i: (i, 0)), full(T, N), full(8, NC, N), full(8, NC, N),
            full(H, N), full(W, N), full(2, NSTR, PAY, N), smem,
        ],
        out_shape=[
            jax.ShapeDtypeStruct((T, CH), BF16), jax.ShapeDtypeStruct((T, N), F32),
            jax.ShapeDtypeStruct((8, NC, N), F32), jax.ShapeDtypeStruct((8, NC, N), F32),
            jax.ShapeDtypeStruct((H, N), F32), jax.ShapeDtypeStruct((W, N), BF16),
            jax.ShapeDtypeStruct((2, NSTR, PAY, N), BF16), jax.ShapeDtypeStruct((16,), jnp.int32),
        ],
        scratch_shapes=[
            pltpu.VMEM((CH // N, BLK + 16, N), F32), pltpu.VMEM((5, N, W), F32),
            pltpu.VMEM((8, CH), F32), pltpu.VMEM((8, T), jnp.int32), pltpu.VMEM((N, T), F32),
            pltpu.VMEM((BLK, W), BF16),
        ],
        compiler_params=pltpu.CompilerParams(dimension_semantics=("arbitrary",)),
        name="first",
    )(bounds, owners, x, halo, cw, cb, ld, dt, ldr, dtr)


def exchange_kernel(
    meta, ends, gate, sends, carried, got,
    seen, seen_gate, prefix, fixed, my_gate,
    s1, r1, s2, r2, s3, r3, s4, r4, own_sem,
):
    me = lax.axis_index("seq")
    st = lax.axis_index("stream")
    barrier = pltpu.get_barrier_semaphore()

    @pl.loop(1, NSEQ)
    def _(k):
        pl.semaphore_signal(
            barrier, inc=1, device_id=(st, lax.rem(me + k, NSEQ)), device_id_type=MESH
        )

    for k in range(1, NSTR):
        pl.semaphore_signal(
            barrier, inc=1, device_id=(lax.rem(st + k, NSTR), me), device_id_type=MESH
        )
    my_gate[...] = jnp.where(meta[12] == 0, gate[...], 0.0)
    pl.semaphore_wait(barrier, NSEQ - 1 + NSTR - 1)

    def handoff(k, slot, src, s, r):
        to = lax.rem(st + k, NSTR)
        return pltpu.make_async_remote_copy(
            src_ref=src.at[to], dst_ref=got.at[slot, st], send_sem=s.at[k], recv_sem=r.at[k],
            device_id=(to, me), device_id_type=MESH,
        )

    def spread(k):
        to = lax.rem(me + k, NSEQ)
        state = pltpu.make_async_remote_copy(
            src_ref=ends.at[to], dst_ref=seen.at[me], send_sem=s1.at[k], recv_sem=r1.at[k],
            device_id=(st, to), device_id_type=MESH,
        )
        factor = pltpu.make_async_remote_copy(
            src_ref=my_gate.at[pl.ds(lax.div(to, 2), 1)], dst_ref=seen_gate.at[pl.ds(me, 1)],
            send_sem=s2.at[k], recv_sem=r2.at[k], device_id=(st, to), device_id_type=MESH,
        )
        return state, factor

    def give(k):
        to = lax.rem(me + k, NSEQ)
        return pltpu.make_async_remote_copy(
            src_ref=prefix.at[to], dst_ref=carried.at[me], send_sem=s1.at[NSEQ + k],
            recv_sem=r1.at[NSEQ + k], device_id=(st, to), device_id_type=MESH,
        )

    for k in range(1, NSEQ):
        state, factor = spread(k)
        factor.start()
        state.start()
    for k in range(1, NSTR):
        handoff(k, 1, sends.at[1], s3, r3).start()
    own = pltpu.make_async_copy(sends.at[1, st], got.at[1, st], own_sem)
    own.start()
    seen[pl.ds(me, 1)] = ends[pl.ds(me, 1)]
    seen_gate[pl.ds(me, 1), :] = my_gate[pl.ds(lax.div(me, 2), 1), :]
    for k in range(1, NSEQ):
        state, factor = spread(k)
        factor.wait()
        state.wait()

    def step(q, state):
        prefix[q] = state.astype(BF16)
        return seen[q].astype(F32) + seen_gate[pl.ds(q, 1), :] * state

    lax.fori_loop(0, NSEQ, step, jnp.zeros((32, N), F32))
    for k in range(1, NSEQ):
        give(k).start()
    carried[pl.ds(me, 1)] = prefix[pl.ds(me, 1)]
    for k in range(1, NSEQ):
        give(k).wait()

    def correct(d, _):
        lift = jnp.where(meta[12] > 0, gate[pl.ds(lax.div(d, 2), 1), :], 0.0)
        extra = carried[d].astype(F32) * lift
        rows = pl.ds(pl.multiple_of(d * 32, 32), 32)
        for o in range(NSTR):
            mine = jnp.where(meta[4] == o, extra, 0.0)
            fixed[o, rows, :] = (sends[0, o, rows, :].astype(F32) + mine).astype(BF16)
        return 0

    lax.fori_loop(0, NSEQ, correct, 0)
    for o in range(NSTR):
        fixed[o, W:PAY, :] = sends[0, o, W:PAY, :]
    for k in range(1, NSTR):
        handoff(k, 0, fixed, s4, r4).start()
    own.wait()
    got[pl.ds(0, 1), pl.ds(st, 1)] = fixed[pl.ds(st, 1)][None]
    for k in range(1, NSTR):
        handoff(k, 1, sends.at[1], s3, r3).wait()
        handoff(k, 0, fixed, s4, r4).wait()


def run_exchange(meta, ends, gate, sends):
    vmem = pl.BlockSpec(memory_space=pltpu.VMEM)
    dma = pltpu.SemaphoreType.DMA
    return pl.pallas_call(
        exchange_kernel,
        in_specs=[pl.BlockSpec(memory_space=pltpu.SMEM), vmem, vmem, vmem],
        out_specs=[vmem, vmem],
        out_shape=[
            jax.ShapeDtypeStruct((NSEQ, 32, N), BF16),
            jax.ShapeDtypeStruct((2, NSTR, PAY, N), BF16),
        ],
        scratch_shapes=[
            pltpu.VMEM((NSEQ, 32, N), BF16), pltpu.VMEM((NSEQ, N), F32),
            pltpu.VMEM((NSEQ, 32, N), BF16), pltpu.VMEM((NSTR, PAY, N), BF16),
            pltpu.VMEM((H, N), F32),
            dma((2 * NSEQ,)), dma((2 * NSEQ,)), dma((NSEQ,)), dma((NSEQ,)),
            dma((NSTR,)), dma((NSTR,)), dma((NSTR,)), dma((NSTR,)), dma,
        ],
        compiler_params=pltpu.CompilerParams(collective_id=0, has_side_effects=True),
        name="exchange",
    )(meta, ends, gate, sends)


def last_kernel(
    meta, skip, act, cols, crow, grow, carried, got,
    out, ssm, tails,
    h, hb, skips,
):
    i = pl.program_id(0)

    @pl.when(i == 0)
    def _():
        lane = iota((L, N), 1)
        for j in range(8):
            gain = jnp.where(lane < L, skip[2 * j], skip[2 * j + 1])
            skips[j] = jnp.where(lane % L == iota((L, N), 0), gain, 0.0).astype(BF16)
            tile = carried[j * N : (j + 1) * N, :].astype(F32).T
            h[:, j * N : (j + 1) * N] = tile
            hb[:, j * N : (j + 1) * N] = tile.astype(BF16)

    @pl.when(i < 8)
    def _():
        ssm[...] = got[0, 0, 0:W, :].astype(F32).reshape(ssm.shape)
        tail = got[0, 0, W:PAY, :].astype(F32)
        for j in range(CH // N):
            for k in range(3):
                row = tail[3 * j + k : 3 * j + k + 1, :].astype(BF16)
                tails[0, 0, k : k + 1, j * N : (j + 1) * N] = row

    part = iota((L, N), 1) // L
    zero = jnp.zeros((L, N), BF16)
    for q in range(BLK // L):
        rows = slice(q * L, (q + 1) * L)
        c = i * (BLK // L) + q
        cmat = act[rows, W + N : CH]
        bmat = act[rows, W : W + N]
        flipped = bmat.T
        col = cols[rows, :]
        score = dot(cmat, jnp.concatenate([bmat, bmat], 0), 1, 1)
        pos = c * L + iota((L, N), 0)
        src = c * L + iota((L, N), 1) % L
        keep = (src <= pos) & (src >= doc_start(pos, meta))
        score = jnp.where(keep, score, 0.0).astype(BF16)
        for g in range(4):
            wide = slice(g * 2 * N, (g + 1) * 2 * N)
            mix, pairs, entry, loads = [], [], [], []
            for j in (2 * g, 2 * g + 1):
                x = act[rows, j * N : (j + 1) * N]
                spread = pick(col, part + 2 * j) - crow[j, pl.ds(c, 1), :]
                mix.append(jnp.exp2(jnp.minimum(spread, 30.0)).astype(BF16) * score + skips[j])
                for half in (0, 1):
                    own = jnp.where(part == half, x, zero)
                    pairs.append(jnp.concatenate([own, zero] if j == 2 * g else [zero, own], 1))
                loads.append(x * pick(col, part + (2 * j + H)).astype(BF16))
                entry.append(pick(col, part + (2 * j + 2 * H)))
            inner = dot(jnp.concatenate(mix, 1), jnp.concatenate(pairs, 0))
            outer = dot(cmat, hb[:, wide]) * jnp.concatenate(entry, 1)
            out[rows, wide] = (inner + outer).astype(BF16)
            fresh = dot(flipped, jnp.concatenate(loads, 1))
            for j in (0, 1):
                lanes = slice((2 * g + j) * N, (2 * g + j + 1) * N)
                state = grow[2 * g + j, pl.ds(c, 1), :] * h[:, lanes] + fresh[:, j * N : (j + 1) * N]
                h[:, lanes] = state
                hb[:, lanes] = state.astype(BF16)


def run_last(meta, skip, act, cols, crow, grow, carried, got):
    smem = pl.BlockSpec(memory_space=pltpu.SMEM)
    full = lambda *shape: pl.BlockSpec(shape, lambda i: (0,) * len(shape))
    slot = lambda i: jnp.minimum(i, 7)
    return pl.pallas_call(
        last_kernel,
        grid=(STEPS,),
        in_specs=[
            smem, smem, pl.BlockSpec((BLK, CH), lambda i: (i, 0)),
            pl.BlockSpec((BLK, N), lambda i: (i, 0)), full(8, NC, N), full(8, NC, N), full(W, N),
            pl.BlockSpec((1, 1, PAY, N), lambda i: (slot(i) % 2, slot(i) // 2, 0, 0)),
        ],
        out_specs=[
            pl.BlockSpec((BLK, W), lambda i: (i, 0)),
            pl.BlockSpec((1, 1, H, L, N), lambda i: (slot(i) // 2, slot(i) % 2, 0, 0, 0)),
            pl.BlockSpec((1, 1, 3, CH), lambda i: (slot(i) // 2, slot(i) % 2, 0, 0)),
        ],
        out_shape=[
            jax.ShapeDtypeStruct((T, W), BF16),
            jax.ShapeDtypeStruct((NSTR, 2, H, L, N), F32),
            jax.ShapeDtypeStruct((NSTR, 2, 3, CH), BF16),
        ],
        scratch_shapes=[
            pltpu.VMEM((N, W), F32), pltpu.VMEM((N, W), BF16), pltpu.VMEM((8, L, N), BF16),
        ],
        compiler_params=pltpu.CompilerParams(dimension_semantics=("arbitrary",)),
        name="last",
    )(meta, skip, act, cols, crow, grow, carried, got)


def by_block(rows):
    return rows.reshape(H, NC, L).transpose(1, 0, 2).reshape(NC, W)


def on_device(x, cw, cb, dt, ld, skip, bounds, owners):
    x, dt, ld = x[0], dt[0], ld[0]
    halo = lax.ppermute(x[T - 16 :], "seq", [(k, k + 1) for k in range(NSEQ - 1)])
    act, cols, crow, grow, gate, ends, sends, meta = run_first(
        bounds[0], owners[0], x, halo, cw, cb[None], ld, dt, by_block(ld), by_block(dt)
    )
    carried, got = run_exchange(meta, ends.reshape(NSEQ, 32, N), gate, sends)
    out, ssm, tails = run_last(
        meta, skip, act, cols, crow, grow, carried.reshape(W, N), got
    )
    return out[None], ssm[None, None], tails[None, None]


def solution(mesh):
    in_specs = (
        P("stream", "seq", None),
        P(),
        P(),
        P("stream", None, "seq"),
        P("stream", None, "seq"),
        P(),
        P("stream", None),
        P("stream", None),
    )
    out_specs = (
        P("stream", "seq", None),
        P("stream", "seq", None, None, None, None, None),
        P("stream", "seq", None, None, None, None),
    )
    return jax.shard_map(
        on_device, mesh=mesh, in_specs=in_specs, out_specs=out_specs, check_vma=False
    )
```

```python
import functools

import jax
import jax.numpy as jnp
from jax import lax
from jax.experimental import pallas as pl
from jax.experimental.pallas import tpu as pltpu
from jax.sharding import PartitionSpec as P

MESH = pl.DeviceIdType.MESH
F32 = jnp.float32
BF16 = jnp.bfloat16
T = 4096
CH = 1280
W = 1024
H = 16
N = 128
L = 64
BLK = 256
STEPS = T // BLK
TALL = 512
NC = T // L
NSEQ = 32
NSTR = 4
PAY = 1056
BIG = 1 << 20
LOG2E = 1.4426950408889634
AT_SEND = 1
AT_SCAN = 4
AT_FIX = 8


def dot(a, b, ca=1, cb=0):
    return lax.dot_general(a, b, (((ca,), (cb,)), ((), ())), preferred_element_type=F32)


def iota(shape, dim):
    return lax.broadcasted_iota(jnp.int32, shape, dim)


def doc_start(pos, meta):
    start = jnp.full(pos.shape, meta[13], jnp.int32)
    for n in range(4):
        start = jnp.where(pos >= meta[n], meta[n], start)
    return start


def doc_end(pos, meta):
    end = jnp.full(pos.shape, T, jnp.int32)
    for n in range(3, -1, -1):
        end = jnp.where(pos < meta[n], jnp.minimum(meta[n], T), end)
    return end


def pick(table, lane):
    return jnp.take_along_axis(table, lane, axis=1)


def left(v, s):
    return pltpu.roll(v, v.shape[1] - s, 1)


def count_upto(bounds, value):
    total = bounds.shape[0]
    found = jnp.int32(0)
    step = total
    while step:
        reach = found + step
        ahead = bounds[jnp.minimum(reach, total) - 1] <= value
        found = jnp.where((reach <= total) & ahead, reach, found)
        step //= 2
    return found


def scan_docs(bounds, owners, meta, anchor):
    for k in range(16):
        meta[k] = BIG if k < 4 else 0
    total = bounds.shape[0]
    low = count_upto(bounds, anchor)
    high = jnp.minimum(count_upto(bounds, anchor + T - 1) + 1, total)
    before = jnp.where(low > 0, bounds[jnp.maximum(low - 1, 0)], 0)
    meta[13] = before - anchor

    def body(k, prev):
        bound = bounds[k]

        @pl.when((bound <= anchor + T) & (bound > prev))
        def _():
            n = meta[12]
            owner = owners[k]
            rank = jnp.int32(0)
            for m in range(4):
                same = (m < n) & (meta[4 + m] == owner)
                rank = rank + jnp.where(same, 1, 0).astype(jnp.int32)
            meta[n] = bound - anchor
            meta[4 + n] = owner
            meta[8 + n] = rank
            meta[12] = n + 1

        return bound

    lax.fori_loop(low, high, body, before)


def document_decay(meta, ld, dt, table, columns, gate):
    pos = iota((1, T), 1)
    end = doc_end(pos, meta)
    for half in range(2):
        heads = slice(8 * half, 8 * half + 8)
        v = ld[heads, :] * LOG2E
        seg = jnp.where(pos + 1 < end, left(v, 1), 0.0)
        for k in range(12):
            s = 1 << k
            seg = seg + jnp.where(pos + s < end, left(seg, s), 0.0)
        whole = jnp.exp2(v[:, :1] + seg[:, :1])
        gate[heads, :] = jnp.broadcast_to(jnp.where(meta[13] < 0, whole, 0.0), (8, N))
        weight = jnp.exp2(seg) * dt[heads, :]
        for b in range(T // TALL):
            at = b * H + 8 * half
            table[at : at + 8, :] = weight[:, b * TALL : (b + 1) * TALL]
    for b in range(TALL // N):
        columns[b * N : (b + 1) * N, :] = table[:, b * N : (b + 1) * N].T


def block_decay(meta, ld, dt, table, keys, cols, crow, grow):
    pos = iota((1, T), 1)
    place = pos % L
    base = pos - place
    ending = doc_end(pos, meta) >= base + L
    open_entry = doc_start(pos, meta) < base
    open_block = doc_start(base + (L - 1), meta) < base
    for half in range(2):
        heads = slice(8 * half, 8 * half + 8)
        v = ld[heads, :] * LOG2E
        suf = jnp.where(place + 1 < L, left(v, 1), 0.0)
        for k in range(6):
            s = 1 << k
            suf = suf + jnp.where(place + s < L, left(suf, s), 0.0)
        weight = jnp.where(ending, jnp.exp2(suf) * dt[heads, :], 0.0)
        keys[H + 8 * half : H + 8 * half + 8, :] = suf
        cum = ld[heads, :] * LOG2E
        for k in range(6):
            s = 1 << k
            cum = cum + jnp.where(place >= s, pltpu.roll(cum, s, 1), 0.0)
        entry = jnp.where(open_entry, jnp.exp2(cum), 0.0)
        for kind, value in enumerate((cum, weight, entry)):
            for b in range(2):
                at = b * 3 * H + kind * H + 8 * half
                table[at : at + 8, :] = value[:, b * (T // 2) : (b + 1) * (T // 2)]
        keys[heads, :] = cum - jnp.log2(dt[heads, :])
        suf = keys[H + 8 * half : H + 8 * half + 8, :]
        keys[H + 8 * half : H + 8 * half + 8, :] = jnp.where(open_block, jnp.exp2(cum + suf), 0.0)
    table[6 * H : N, :] = jnp.zeros((N - 6 * H, T // 2), F32)
    for b in range(T // 2 // N):
        cols[b * N : (b + 1) * N, :] = table[:, b * N : (b + 1) * N].T
    low_lane = iota((T // N, N), 1) < L
    for j in range(8):
        for row, out in ((2 * j, crow), (H + 2 * j, grow)):
            first = keys[row : row + 1, :].reshape(T // N, N)
            second = keys[row + 1 : row + 2, :].reshape(T // N, N)
            out[j, 0 : T // N, :] = jnp.where(low_lane, first, pltpu.roll(second, L, 1))
            out[j, T // N :, :] = jnp.where(low_lane, pltpu.roll(first, L, 1), second)


def block_row(c):
    return (c & 1) * (T // N) + (c >> 1)


def first_kernel(
    bounds, owners, x_ref, halo, cw, cb, ld, dt,
    act, gate, ends, sends, meta,
    xf, acc, half, table, cols, load, weights, flipped, held,
):
    i = pl.program_id(0)
    anchor = lax.axis_index("seq") * T

    @pl.when(i == 0)
    def _():
        scan_docs(bounds, owners, meta, anchor)
        document_decay(meta, ld, dt, table, cols, gate)
        acc[...] = jnp.zeros_like(acc)
        sends[...] = jnp.zeros_like(sends)
        load[...] = jnp.zeros_like(load)
        flipped[...] = jnp.zeros_like(flipped)
        held[0] = 0
        half[0:4, :] = cw[...] * 0.5
        before = iota((16, 1), 0) - 16
        real = (before >= meta[13]) & (anchor > 0)
        for j in range(CH // N):
            half[4:5, j * N : (j + 1) * N] = cb[pl.ds(j * N, N)].reshape(1, N) * 0.5
            rows = halo[:, j * N : (j + 1) * N].astype(F32)
            xf[j, 0:16, :] = jnp.where(real, rows, 0.0)

    def gather(j, lag_sum):
        lanes = slice(j * N, (j + 1) * N)
        v = half[4:5, lanes] + half[0:1, lanes] * lag_sum(0)
        for k in range(1, 4):
            v = v + half[k : k + 1, lanes] * lag_sum(k)
        return (v + v * jnp.tanh(v)).astype(BF16)

    def add_segment(j):
        for g in range(4):
            lanes = slice(g * 2 * N, (g + 1) * 2 * N)
            acc[j, :, lanes] = acc[j, :, lanes] + dot(flipped[...], load[:, lanes])

    add_segment(held[0])
    part = iota((L, N), 1) // L
    for j in range(CH // N):
        xf[j, 16 : 16 + BLK, :] = x_ref[:, j * N : (j + 1) * N].astype(F32)
        for r in range(0, BLK, L):
            lagged = lambda k: xf[j, 16 + r - k : 16 + L + r - k, :]
            act[r : r + L, j * N : (j + 1) * N] = gather(j, lagged)
            if j < 8:
                col = cols[pl.ds(pl.multiple_of((i & 1) * BLK + r, L), L), :]
                weight = pick(col, part + (2 * j + H * (i >> 1))).astype(BF16)
                weights[r : r + L, j * N : (j + 1) * N] = weight

    def fix(m, _):
        doc_begin = meta[m >> 1]
        group = (doc_begin + 2 * (m & 1)) >> 4
        again = ((m & 1) == 1) & (group == doc_begin >> 4)

        @pl.when((group >> 4 == i) & jnp.logical_not(again))
        def _():
            at = pl.multiple_of((group & 15) * 16, 16)
            pos = group * 16 + iota((16, 1), 0)
            start = doc_start(pos, meta)
            for j in range(CH // N):
                rows = xf[j, pl.ds(at, 32), :]
                lagged = lambda k: jnp.where(pos - k >= start, rows[16 - k : 32 - k], 0.0)
                act[pl.ds(at, 16), j * N : (j + 1) * N] = gather(j, lagged)

        return 0

    def take_tail(n, _):
        last = meta[n] - 1

        @pl.when(last >> 8 == i)
        def _():
            row = iota((32, 16 + BLK), 0)
            at = iota((32, 16 + BLK), 1) - 16 + i * BLK
            begin = jnp.where(n > 0, meta[jnp.maximum(n - 1, 0)], meta[13])
            total = jnp.zeros((32, N), F32)
            for j in range(CH // N):
                lag = row - 3 * j
                hit = (lag >= 0) & (lag < 3) & (at == last - 2 + lag) & (at >= begin)
                total = total + dot(jnp.where(hit, 1.0, 0.0).astype(BF16), xf[j].astype(BF16))
            sends[meta[8 + n], meta[4 + n], W:PAY, :] = total.astype(BF16)

        return 0

    touched = jnp.bool_(False)
    for n in range(4):
        touched = touched | ((meta[n] - 1) >> 8 == i) | ((meta[n] + 2) >> 8 == i)

    @pl.when(touched)
    def _():
        lax.fori_loop(0, 8, fix, 0)
        lax.fori_loop(0, 4, take_tail, 0)

    low = jnp.int32(0)
    high = jnp.int32(0)
    for n in range(4):
        low = low + jnp.where(meta[n] <= i * BLK, 1, 0).astype(jnp.int32)
        high = high + jnp.where(meta[n] <= i * BLK + BLK - 1, 1, 0).astype(jnp.int32)
    row = i * BLK + iota((BLK, 1), 0)

    def flip(j):
        begin = jnp.where(j > 0, meta[jnp.maximum(j - 1, 0)], 0)
        stop = jnp.where(j < 4, meta[jnp.minimum(j, 3)], BIG)
        kept = jnp.where((row >= begin) & (row < stop), act[:, W : W + N].astype(F32), 0.0)
        flipped[...] = kept.astype(BF16).T

    for j in range(CH // N):
        xf[j, 0:16, :] = xf[j, BLK : BLK + 16, :]
    load[...] = act[:, 0:W] * weights[...]

    def segment(j, _):
        flip(j)
        add_segment(j)
        return 0

    lax.fori_loop(low, high, segment, 0)
    flip(high)
    held[0] = high

    @pl.when(i == STEPS - 1)
    def _():
        add_segment(held[0])
        for b in range(8):
            tile = acc[meta[12], :, b * N : (b + 1) * N].T
            ends[b * N : (b + 1) * N, :] = tile.astype(BF16)

        def put(n, _):
            for b in range(8):
                tile = acc[n, :, b * N : (b + 1) * N].T
                sends[meta[8 + n], meta[4 + n], b * N : (b + 1) * N, :] = tile.astype(BF16)
            return 0

        lax.fori_loop(0, meta[12], put, 0)


def run_first(bounds, owners, x, halo, cw, cb, ld, dt):
    smem = pl.BlockSpec(memory_space=pltpu.SMEM)
    full = lambda *shape: pl.BlockSpec(shape, lambda i: (0,) * len(shape))
    return pl.pallas_call(
        first_kernel,
        grid=(STEPS,),
        in_specs=[
            smem, smem, pl.BlockSpec((BLK, CH), lambda i: (i, 0)), full(16, CH), full(4, CH),
            full(CH), full(H, T), full(H, T),
        ],
        out_specs=[
            pl.BlockSpec((BLK, CH), lambda i: (i, 0)), full(H, N), full(W, N), full(2, NSTR, PAY, N), smem,
        ],
        out_shape=[
            jax.ShapeDtypeStruct((T, CH), BF16),
            jax.ShapeDtypeStruct((H, N), F32), jax.ShapeDtypeStruct((W, N), BF16),
            jax.ShapeDtypeStruct((2, NSTR, PAY, N), BF16), jax.ShapeDtypeStruct((16,), jnp.int32),
        ],
        scratch_shapes=[
            pltpu.VMEM((CH // N, BLK + 16, N), F32), pltpu.VMEM((5, N, W), F32),
            pltpu.VMEM((8, CH), F32), pltpu.VMEM((N, TALL), F32), pltpu.VMEM((TALL, N), F32),
            pltpu.VMEM((BLK, W), BF16),
            pltpu.VMEM((BLK, W), BF16), pltpu.VMEM((N, BLK), BF16), pltpu.SMEM((1,), jnp.int32),
        ],
        compiler_params=pltpu.CompilerParams(dimension_semantics=("arbitrary",)),
        name="first",
    )(bounds, owners, x, halo, cw, cb, ld, dt)


def middle_kernel(
    meta, skip, act, ld, dt, ends, gate, sends,
    out, cols, grow, carried_out, got,
    h, hb, skips, crow, table, keys, seen, seen_gate, prefix, carried, fixed, my_gate,
    s1, r1, s2, r2, s3, r3, s4, r4, own_sem,
):
    i = pl.program_id(0)
    me = lax.axis_index("seq")
    st = lax.axis_index("stream")

    def handoff(k, slot, src, s, r):
        to = lax.rem(st + k, NSTR)
        return pltpu.make_async_remote_copy(
            src_ref=src.at[to], dst_ref=got.at[slot, st], send_sem=s.at[k], recv_sem=r.at[k],
            device_id=(to, me), device_id_type=MESH,
        )

    def spread(k):
        to = lax.rem(me + k, NSEQ)
        state = pltpu.make_async_remote_copy(
            src_ref=ends.at[to], dst_ref=seen.at[me], send_sem=s1.at[k], recv_sem=r1.at[k],
            device_id=(st, to), device_id_type=MESH,
        )
        factor = pltpu.make_async_remote_copy(
            src_ref=my_gate.at[pl.ds(lax.div(to, 2), 1)], dst_ref=seen_gate.at[pl.ds(me, 1)],
            send_sem=s2.at[k], recv_sem=r2.at[k], device_id=(st, to), device_id_type=MESH,
        )
        return state, factor

    def give(k):
        to = lax.rem(me + k, NSEQ)
        return pltpu.make_async_remote_copy(
            src_ref=prefix.at[to], dst_ref=carried.at[me], send_sem=s1.at[NSEQ + k],
            recv_sem=r1.at[NSEQ + k], device_id=(st, to), device_id_type=MESH,
        )

    def keep_own(slot, src):
        return pltpu.make_async_copy(src.at[st], got.at[slot, st], own_sem.at[slot])

    @pl.when(i == 0)
    def _():
        barrier = pltpu.get_barrier_semaphore()

        @pl.loop(1, NSEQ)
        def _(k):
            pl.semaphore_signal(
                barrier, inc=1, device_id=(st, lax.rem(me + k, NSEQ)), device_id_type=MESH
            )

        for k in range(1, NSTR):
            pl.semaphore_signal(
                barrier, inc=1, device_id=(lax.rem(st + k, NSTR), me), device_id_type=MESH
            )
        my_gate[...] = jnp.where(meta[12] == 0, gate[...], 0.0)
        block_decay(meta, ld, dt, table, keys, cols, crow, grow)
        h[...] = jnp.zeros_like(h)
        hb[...] = jnp.zeros_like(hb)
        lane = iota((L, N), 1)
        for j in range(8):
            gain = jnp.where(lane < L, skip[2 * j], skip[2 * j + 1])
            skips[j] = jnp.where(lane % L == iota((L, N), 0), gain, 0.0).astype(BF16)

    @pl.when(i == AT_SEND)
    def _():
        pl.semaphore_wait(pltpu.get_barrier_semaphore(), NSEQ - 1 + NSTR - 1)

        @pl.loop(1, NSEQ)
        def _(k):
            state, factor = spread(k)
            factor.start()
            state.start()

        for k in range(1, NSTR):
            handoff(k, 1, sends.at[1], s3, r3).start()
        keep_own(1, sends.at[1]).start()
        seen[pl.ds(me, 1)] = ends[pl.ds(me, 1)]
        seen_gate[pl.ds(me, 1), :] = my_gate[pl.ds(lax.div(me, 2), 1), :]

    @pl.when(i == AT_SCAN)
    def _():
        @pl.loop(1, NSEQ)
        def _(k):
            state, factor = spread(k)
            factor.wait()
            state.wait()

        def step(q, state):
            prefix[q] = state.astype(BF16)
            return seen[q].astype(F32) + seen_gate[pl.ds(q, 1), :] * state

        lax.fori_loop(0, NSEQ, step, jnp.zeros((32, N), F32), unroll=8)

        @pl.loop(1, NSEQ)
        def _(k):
            give(k).start()

        carried[pl.ds(me, 1)] = prefix[pl.ds(me, 1)]

    @pl.when(i == AT_FIX)
    def _():
        @pl.loop(1, NSEQ)
        def _(k):
            give(k).wait()

        def correct(d, _):
            lift = jnp.where(meta[12] > 0, gate[pl.ds(lax.div(d, 2), 1), :], 0.0)
            extra = carried[d].astype(F32) * lift
            rows = pl.ds(pl.multiple_of(d * 32, 32), 32)
            for o in range(NSTR):
                mine = jnp.where(meta[4] == o, extra, 0.0)
                fixed[o, rows, :] = (sends[0, o, rows, :].astype(F32) + mine).astype(BF16)
            return 0

        lax.fori_loop(0, NSEQ, correct, 0, unroll=8)
        for o in range(NSTR):
            fixed[o, W:PAY, :] = sends[0, o, W:PAY, :]
        for k in range(1, NSTR):
            handoff(k, 0, fixed, s4, r4).start()
        keep_own(0, fixed).start()
        carried_out[...] = carried[...]

    part = iota((L, N), 1) // L
    lane = part + 3 * H * (i >> 3)
    zero = jnp.zeros((L, N), BF16)
    for q in range(BLK // L):
        rows = slice(q * L, (q + 1) * L)
        c = i * (BLK // L) + q
        cmat = act[rows, W + N : CH]
        bmat = act[rows, W : W + N]
        flipped = bmat.T
        at = (i & (STEPS // 2 - 1)) * BLK + q * L
        col = cols[pl.ds(pl.multiple_of(at, L), L), :]
        score = dot(cmat, jnp.concatenate([bmat, bmat], 0), 1, 1)
        pos = c * L + iota((L, N), 0)
        src = c * L + iota((L, N), 1) % L
        keep = (src <= pos) & (src >= doc_start(pos, meta))
        score = jnp.where(keep, score, 0.0).astype(BF16)
        for g in range(4):
            wide = slice(g * 2 * N, (g + 1) * 2 * N)
            mix, pairs, entry, loads = [], [], [], []
            for j in (2 * g, 2 * g + 1):
                x = act[rows, j * N : (j + 1) * N]
                spread = pick(col, lane + 2 * j) - crow[j, pl.ds(block_row(c), 1), :]
                mix.append(jnp.exp2(jnp.minimum(spread, 30.0)).astype(BF16) * score + skips[j])
                for half in (0, 1):
                    own = jnp.where(part == half, x, zero)
                    pairs.append(jnp.concatenate([own, zero] if j == 2 * g else [zero, own], 1))
                loads.append(x * pick(col, lane + (2 * j + H)).astype(BF16))
                entry.append(pick(col, lane + (2 * j + 2 * H)))
            inner = dot(jnp.concatenate(mix, 1), jnp.concatenate(pairs, 0))
            outer = dot(cmat, hb[:, wide]) * jnp.concatenate(entry, 1)
            out[rows, wide] = (inner + outer).astype(BF16)
            fresh = dot(flipped, jnp.concatenate(loads, 1))
            for j in (0, 1):
                lanes = slice((2 * g + j) * N, (2 * g + j + 1) * N)
                state = grow[2 * g + j, pl.ds(block_row(c), 1), :] * h[:, lanes] + fresh[:, j * N : (j + 1) * N]
                h[:, lanes] = state
                hb[:, lanes] = state.astype(BF16)

    @pl.when(i == STEPS - 1)
    def _():
        keep_own(1, sends.at[1]).wait()
        keep_own(0, fixed).wait()
        for k in range(1, NSTR):
            handoff(k, 1, sends.at[1], s3, r3).wait()
            handoff(k, 0, fixed, s4, r4).wait()


def run_middle(meta, skip, act, ld, dt, ends, gate, sends):
    smem = pl.BlockSpec(memory_space=pltpu.SMEM)
    full = lambda *shape: pl.BlockSpec(shape, lambda i: (0,) * len(shape))
    dma = pltpu.SemaphoreType.DMA
    return pl.pallas_call(
        middle_kernel,
        grid=(STEPS,),
        in_specs=[
            smem, smem, pl.BlockSpec((BLK, CH), lambda i: (i, 0)),
            full(H, T), full(H, T),
            full(NSEQ, 32, N), full(H, N), full(2, NSTR, PAY, N),
        ],
        out_specs=[
            pl.BlockSpec((BLK, W), lambda i: (i, 0)), full(T // 2, N), full(8, NC, N),
            full(NSEQ, 32, N), pl.BlockSpec(memory_space=pl.ANY),
        ],
        out_shape=[
            jax.ShapeDtypeStruct((T, W), BF16), jax.ShapeDtypeStruct((T // 2, N), F32),
            jax.ShapeDtypeStruct((8, NC, N), F32),
            jax.ShapeDtypeStruct((NSEQ, 32, N), BF16),
            jax.ShapeDtypeStruct((2, NSTR, PAY, N), BF16),
        ],
        scratch_shapes=[
            pltpu.VMEM((N, W), F32), pltpu.VMEM((N, W), BF16), pltpu.VMEM((8, L, N), BF16),
            pltpu.VMEM((8, NC, N), F32), pltpu.VMEM((N, T // 2), F32), pltpu.VMEM((2 * H, T), F32),
            pltpu.VMEM((NSEQ, 32, N), BF16), pltpu.VMEM((NSEQ, N), F32),
            pltpu.VMEM((NSEQ, 32, N), BF16), pltpu.VMEM((NSEQ, 32, N), BF16),
            pltpu.VMEM((NSTR, PAY, N), BF16), pltpu.VMEM((H, N), F32),
            dma((2 * NSEQ,)), dma((2 * NSEQ,)), dma((NSEQ,)), dma((NSEQ,)),
            dma((NSTR,)), dma((NSTR,)), dma((NSTR,)), dma((NSTR,)), dma((2,)),
        ],
        compiler_params=pltpu.CompilerParams(
            collective_id=0, has_side_effects=True, dimension_semantics=("arbitrary",)
        ),
        name="middle",
    )(meta, skip, act, ld, dt, ends, gate, sends)


def last_kernel(meta, partial, cmats, cols, grow, carried, got, out, ssm, tails, turned, through):
    i = pl.program_id(0)

    @pl.when(i == 0)
    def _():
        through[...] = jnp.ones_like(through)
        for j in range(8):
            turned[:, j * N : (j + 1) * N] = carried[j * N : (j + 1) * N, :].T

    @pl.when(i < 2 * NSTR)
    def _():
        ssm[...] = got[0, 0, 0:W, :].astype(F32).reshape(ssm.shape)
        tail = got[0, 0, W:PAY, :].astype(F32)
        for j in range(CH // N):
            for k in range(3):
                row = tail[3 * j + k : 3 * j + k + 1, :].astype(BF16)
                tails[0, 0, k : k + 1, j * N : (j + 1) * N] = row

    inside = (meta[13] < 0) & (i * TALL < meta[0])

    @pl.when(jnp.logical_not(inside))
    def _():
        out[...] = partial[...]

    @pl.when(inside)
    def _():
        part = iota((TALL, N), 1) // L + 3 * H * (i // (T // 2 // TALL))
        for j in range(8):
            lanes = slice(j * N, (j + 1) * N)
            if j % 2 == 0:
                extra = dot(cmats[...], turned[:, j * N : (j + 2) * N])
            here = through[j]
            for q in range(TALL // L):
                rows = slice(q * L, (q + 1) * L)
                factor = pick(cols[rows, :], part[rows] + (2 * j + 2 * H)) * here
                half = extra[rows, (j % 2) * N : (j % 2 + 1) * N]
                out[rows, lanes] = (partial[rows, lanes].astype(F32) + factor * half).astype(BF16)
                here = here * grow[j, pl.ds(block_row(i * (TALL // L) + q), 1), :]
            through[j] = here


def run_last(meta, partial, act, cols, grow, carried, got):
    smem = pl.BlockSpec(memory_space=pltpu.SMEM)
    full = lambda *shape: pl.BlockSpec(shape, lambda i: (0,) * len(shape))
    slot = lambda i: jnp.minimum(i, 7)
    return pl.pallas_call(
        last_kernel,
        grid=(T // TALL,),
        in_specs=[
            smem, pl.BlockSpec((TALL, W), lambda i: (i, 0)),
            pl.BlockSpec((TALL, N), lambda i: (i, CH // N - 1)),
            pl.BlockSpec((TALL, N), lambda i: (i % (T // 2 // TALL), 0)), full(8, NC, N), full(W, N),
            pl.BlockSpec((1, 1, PAY, N), lambda i: (slot(i) % 2, slot(i) // 2, 0, 0)),
        ],
        out_specs=[
            pl.BlockSpec((TALL, W), lambda i: (i, 0)),
            pl.BlockSpec((1, 1, H, L, N), lambda i: (slot(i) // 2, slot(i) % 2, 0, 0, 0)),
            pl.BlockSpec((1, 1, 3, CH), lambda i: (slot(i) // 2, slot(i) % 2, 0, 0)),
        ],
        out_shape=[
            jax.ShapeDtypeStruct((T, W), BF16),
            jax.ShapeDtypeStruct((NSTR, 2, H, L, N), F32),
            jax.ShapeDtypeStruct((NSTR, 2, 3, CH), BF16),
        ],
        scratch_shapes=[pltpu.VMEM((N, W), BF16), pltpu.VMEM((8, 1, N), F32)],
        compiler_params=pltpu.CompilerParams(dimension_semantics=("arbitrary",)),
        name="last",
    )(meta, partial, act, cols, grow, carried, got)


def on_device(x, cw, cb, dt, ld, skip, bounds, owners):
    x, dt, ld = x[0], dt[0], ld[0]
    halo = lax.ppermute(x[T - 16 :], "seq", [(k, k + 1) for k in range(NSEQ - 1)])
    act, gate, ends, sends, meta = run_first(
        bounds[0], owners[0], x, halo, cw, cb, ld, dt
    )
    partial, cols, grow, carried, got = run_middle(
        meta, skip, act, ld, dt, ends.reshape(NSEQ, 32, N), gate, sends
    )
    out, ssm, tails = run_last(meta, partial, act, cols, grow, carried.reshape(W, N), got)
    return out[None], ssm[None, None], tails[None, None]


def solution(mesh):
    in_specs = (
        P("stream", "seq", None),
        P(),
        P(),
        P("stream", None, "seq"),
        P("stream", None, "seq"),
        P(),
        P("stream", None),
        P("stream", None),
    )
    out_specs = (
        P("stream", "seq", None),
        P("stream", "seq", None, None, None, None, None),
        P("stream", "seq", None, None, None, None),
    )
    return jax.shard_map(
        on_device, mesh=mesh, in_specs=in_specs, out_specs=out_specs, check_vma=False
    )
```
